768 devices in a mesh: seq: 96 (over z_lo, y, x), head: 8 (over z_hi, core).
Axes of the slice: x: 4, y: 8, z: 12 (z_hi: 4, z_lo: 3; z = z_hi * 3 + z_lo), core: 2. Of those that a mesh axis runs over, the one named last changes fastest.
Arguments:
- queries: bfloat16 [12288, 64, 576], P('seq', 'head'), may hold values from -0.06982422 to 0.06982422
- out_grad: bfloat16 [12288, 64, 512], P('seq', 'head'), may hold values from -12 to 12
- latents: bfloat16 [73728, 576], P('seq'), may hold values from -1.6953125 to 1.6953125
- log_norm: bfloat16 [12288, 64], P('seq', 'head'), may hold values from 0 to 12, as said below
- out_delta: bfloat16 [12288, 64], P('seq', 'head'), may hold values from -4 to 4
- plan: int32 [96, 2], P('seq'), may hold values from 0 to 1
Outputs:
- query_out: bfloat16 [12288, 64, 576], P('seq', 'head')
- latent_out: bfloat16 [73728, 576], P(('seq', 'head'))
The draws below stay inside these ranges and needn't reach their ends.
Inputs may be any that keep to these rules, and one draw needn't show every extreme that they name: plan[k, t] names which of the 2 latent blocks of shard k the queries of shard k + t (modulo the shards) visit at step t. log_norm lies within one unit of the log of 768.
All inputs are finite; a program needn't handle non-finite values.
Results may differ from the reference program's by a relative error of at most 0.0049.
Values may be sent and summed in bfloat16 or wider, within the bound.
A program may use at most 32 MiB of HBM per device.

```python
import jax
import jax.numpy as jnp
from jax import lax

LAT = 512
KW = 576
HEADS = 64
PACKET = 128
BLOCK = 384
RES_BLOCKS = 2
TICKS = 2
SHARD = 768
TOKENS = 73728
QROWS = 12288
N_SEQ = 96


def draw_log_norm(key, part):
    centre = jnp.log(jnp.float32(TICKS * BLOCK))
    offset = jax.random.uniform(key, (QROWS, HEADS), jnp.float32, -0.4, 0.4)
    return (centre + offset).astype(jnp.bfloat16)


def with_ends(values, rng, least, top_value):
    longest = values.shape.index(max(values.shape))
    spots = []
    for shift in (0, 1):
        where = [jax.random.randint(jax.random.fold_in(rng, axis), (), 0, length) for axis, length in enumerate(values.shape)]
        where[longest] = (where[longest] + shift) % values.shape[longest]
        spots.append(tuple(where))
    return values.at[spots[0]].set(least).at[spots[1]].set(top_value)


def steps_of(stream_key, dims, cuts, smallest, largest):
    def one(axis_at, shards_of):
        heights = jax.random.uniform(jax.random.fold_in(jax.random.fold_in(stream_key, 6), axis_at), (shards_of,), jnp.float32, smallest / len(cuts), largest / len(cuts))
        return jnp.repeat(jnp.exp(heights), dims[axis_at] // shards_of).reshape((-1,) + (1,) * (len(dims) - axis_at - 1))

    gain = one(*cuts[0])
    for cut in cuts[1:]:
        gain = gain * one(*cut)
    return gain


def noise(stream_key, dims, spread, reach, pieces=(), kind=jnp.bfloat16):
    drawn = jax.random.normal(stream_key, dims, jnp.float32) * spread
    if len(pieces) > 0:
        drawn = steps_of(stream_key, dims, pieces, -0.22, 0.18) * drawn
    return jnp.clip(drawn, min=-reach, max=reach).astype(kind)


def setup_inputs(seed: int = 0) -> dict:
    keys = jax.random.split(jax.random.key(seed), 7)
    queries = jnp.clip(jax.random.uniform(keys[0], (QROWS, HEADS, KW), jnp.float32, -0.06982422, 0.06982422) * steps_of(keys[0], (QROWS, HEADS, KW), ((0, 96), (1, 8)), -0.4, 0.0), -0.06982422, 0.06982422).astype(jnp.bfloat16)
    out_grad = noise(keys[1], (QROWS, HEADS, LAT), 2.0, 12.0, ((0, 96), (1, 8)))
    latents = jnp.clip(jax.random.uniform(keys[2], (TOKENS, KW), jnp.float32, -1.6953125, 1.6953125) * steps_of(keys[2], (TOKENS, KW), ((0, 96),), -0.4, 0.0), -1.6953125, 1.6953125).astype(jnp.bfloat16)
    log_norm = draw_log_norm(jax.random.fold_in(keys[6], 71), 0)
    out_delta = noise(keys[4], (QROWS, HEADS), 1.0, 4.0, ((0, 96), (1, 8)))
    plan = with_ends(jax.random.randint(keys[5], (N_SEQ, TICKS), 0, RES_BLOCKS), jax.random.fold_in(keys[5], 1), 0, RES_BLOCKS - 1).astype(jnp.int32)
    return {"queries": queries, "out_grad": out_grad, "latents": latents, "log_norm": log_norm, "out_delta": out_delta, "plan": plan}


def visit(query_rows, grad_rows, norm_rows, delta_rows, key_rows, q_start, k_start):
    query_f = query_rows.astype(jnp.float32)
    grad_f = grad_rows.astype(jnp.float32)
    key_f = key_rows.astype(jnp.float32)
    scores = jnp.einsum("phc,jc->hpj", query_f, key_f)
    q_pos = q_start + jnp.arange(query_rows.shape[0], dtype=jnp.int32)
    k_pos = k_start + jnp.arange(key_rows.shape[0], dtype=jnp.int32)
    visible = k_pos[None, :] <= q_pos[:, None]
    norm_t = norm_rows.astype(jnp.float32).T[:, :, None]
    attn_prob = jnp.where(visible[None], jnp.exp(scores - norm_t), 0.0)
    prob_grad = jnp.einsum("phl,jl->hpj", grad_f, key_f[:, :LAT])
    delta_t = delta_rows.astype(jnp.float32).T[:, :, None]
    score_low = lax.optimization_barrier((attn_prob * (prob_grad - delta_t)).astype(jnp.bfloat16))
    prob_low = lax.optimization_barrier(attn_prob.astype(jnp.bfloat16))
    score_f = score_low.astype(jnp.float32)
    query_grad = jnp.einsum("hpj,jc->phc", score_f, key_f)
    key_grad = jnp.einsum("hpj,phc->jc", score_f, query_f)
    value_grad = jnp.einsum("hpj,phl->jl", prob_low.astype(jnp.float32), grad_f)
    key_grad = key_grad + jnp.pad(value_grad, ((0, 0), (0, key_rows.shape[1] - LAT)))
    return query_grad, key_grad


def reference(queries, out_grad, latents, log_norm, out_delta, plan):
    shards = N_SEQ
    head_count = queries.shape[1]
    width = queries.shape[2]
    query_blocks = queries.reshape(shards, PACKET, head_count, width)
    grad_blocks = out_grad.reshape(shards, PACKET, head_count, LAT)
    norm_blocks = log_norm.reshape(shards, PACKET, head_count)
    delta_blocks = out_delta.reshape(shards, PACKET, head_count)
    latent_blocks = latents.reshape(shards, RES_BLOCKS, BLOCK, width)

    def per_shard(shard_no):
        query_acc = jnp.zeros((PACKET, head_count, width), jnp.float32)
        key_parts = []
        for tick_no in range(TICKS):
            key_shard = (shard_no - tick_no) % shards
            block_no = plan[key_shard, tick_no]
            key_rows = latent_blocks[key_shard, block_no]
            q_start = shard_no * SHARD + SHARD - PACKET
            k_start = key_shard * SHARD + block_no * BLOCK
            query_grad, key_grad = visit(query_blocks[shard_no], grad_blocks[shard_no], norm_blocks[shard_no], delta_blocks[shard_no], key_rows, q_start, k_start)
            query_acc = query_acc + query_grad
            key_parts.append(key_grad)
        return query_acc.astype(jnp.bfloat16), jnp.stack(key_parts)

    query_out, key_parts = lax.map(per_shard, jnp.arange(shards, dtype=jnp.int32))
    latent_acc = jnp.zeros((shards, RES_BLOCKS, BLOCK, width), jnp.float32)
    for tick_no in range(TICKS):
        rolled = jnp.roll(key_parts[:, tick_no], -tick_no, axis=0)
        picked = (plan[:, tick_no][:, None] == jnp.arange(RES_BLOCKS, dtype=jnp.int32)[None, :]).astype(jnp.float32)
        latent_acc = latent_acc + picked[:, :, None, None] * rolled[:, None]
    return query_out.reshape(queries.shape), latent_acc.reshape(latents.shape).astype(jnp.bfloat16)
```

```python
import jax
import jax.numpy as jnp
from jax import lax
from jax.experimental import pallas as pl
from jax.experimental.pallas import tpu as pltpu
from jax.sharding import PartitionSpec as P

LAT = 512
KW = 576
PACKET = 128
BLOCK = 384
SHARD = 768
CH = BLOCK // 2
QTR = BLOCK // 4
HALF = QTR // 2
F = jnp.float32
B = jnp.bfloat16
MESH = pl.DeviceIdType.MESH
NT = (((1,), (1,)), ((), ()))
NN = (((1,), (0,)), ((), ()))


def dot(a, b, dims):
    return lax.dot_general(a, b, dims, preferred_element_type=F)


def kernel(
    shards, plan, nrm, dlt, q_hbm, do_hbm, lat_hbm, dq_hbm, out,
    qt, dob, do32, do2, own, lt, lr, snd, ds, pt, gbuf, gown, psnd, prcv,
    xs, xr, acc, osb, sab, esb, lsb, mrb, early, late, dqb, lsem, ssem, rsem,
):
    s = lax.axis_index("seq")
    head = lax.axis_index("head")
    z = head // 2
    c = head % 2
    nxt = lax.rem(s + 1, shards)
    prv = lax.rem(s + shards - 1, shards)
    mate = 2 * z + 1 - c

    def chip(zz):
        return 2 * lax.rem(zz + 4, 4) + c

    def remote(src, dst, i, j, seq, hd):
        return pltpu.make_async_remote_copy(
            src_ref=src, dst_ref=dst, send_sem=ssem.at[i], recv_sem=rsem.at[j],
            device_id=(seq, hd), device_id_type=MESH,
        )

    loads = [pltpu.make_async_copy(lat_hbm, own, lsem.at[0]), pltpu.make_async_copy(do_hbm, dob, lsem.at[1])]
    for h in range(8):
        loads.append(pltpu.make_async_copy(q_hbm.at[h], qt.at[:, h * PACKET : (h + 1) * PACKET], lsem.at[2 + h]))
    for load in loads:
        load.start()
    barrier = pltpu.get_barrier_semaphore()
    for there in ((nxt, head), (prv, head), (s, mate), (s, chip(z + 1)), (s, chip(z - 1))):
        pl.semaphore_signal(barrier, inc=1, device_id=there, device_id_type=MESH)

    loads[0].wait()
    rows = pl.ds(pl.multiple_of(c * (KW // 2), 32), KW // 2)
    b0 = plan[0, 0]
    b1 = plan[0, 1]
    w0 = b0.astype(F)
    w1 = b1.astype(F)

    def pick(w, x0, x1):
        return x0.astype(F) * (1.0 - w) + x1.astype(F) * w

    snd[...] = pick(w1, own[rows, :BLOCK], own[rows, BLOCK:]).astype(B)
    lt[:, :BLOCK] = pick(w0, own[:, :BLOCK], own[:, BLOCK:]).astype(B)
    pl.semaphore_wait(barrier, 5)
    spans = ((0, 256), (256, 128))
    send_lat = [
        remote(snd.at[:, pl.ds(a, w)], lt.at[rows, pl.ds(BLOCK + a, w)], i, i, nxt, head)
        for i, (a, w) in enumerate(spans)
    ]
    fwd_lat = [
        remote(lt.at[rows, pl.ds(BLOCK + a, w)], lt.at[rows, pl.ds(BLOCK + a, w)], 2 + i, 2 + i, s, mate)
        for i, (a, w) in enumerate(spans)
    ]
    for copy in send_lat:
        copy.start()

    lr[:BLOCK, :] = lt[:, :BLOCK].T
    loads[1].wait()
    for i in range(4):
        do32[i] = dob[:, :, i * 128 : (i + 1) * 128].astype(F).reshape(8 * PACKET, 128)
    for h in range(8):
        for i in range(4):
            do2[h * PACKET : (h + 1) * PACKET, i * 128 : (i + 1) * 128] = do32[i, pl.ds(h, PACKET, stride=8), :].astype(B)
    for load in loads[2:]:
        load.wait()

    def pair(i):
        return remote(psnd.at[i], prcv.at[i], 4 + i, 4 + i, s, mate)

    def chunk(t, m):
        k0 = t * BLOCK + m * CH
        k = lr[k0 : k0 + CH, :]
        if t == 0 and m == 1:
            key = lax.broadcasted_iota(jnp.int32, (CH, PACKET), 0) + CH
            query = lax.broadcasted_iota(jnp.int32, (CH, PACKET), 1) + (SHARD - PACKET - b0 * BLOCK)
            seen = key <= query
        for g in range(4):
            cols = slice(g * 256, (g + 1) * 256)
            score = dot(k, qt[:, cols], NN)
            grad = dot(k[:, :LAT], do2[cols, :], NT)
            for i in range(2):
                h = 2 * g + i
                part = slice(i * PACKET, (i + 1) * PACKET)
                to = slice(h * PACKET, (h + 1) * PACKET)
                norm = nrm[h : h + 1, :].astype(F)
                if t == 1:
                    norm = norm + jnp.where(s == 0, 1e30, 0.0).astype(F)
                prob = jnp.exp(score[:, part] - norm)
                if t == 0 and m == 1:
                    prob = jnp.where(seen, prob, 0.0)
                ds[k0 : k0 + CH, to] = (prob * (grad[:, part] - dlt[h : h + 1, :].astype(F))).astype(B)
                pt[:, to] = prob.astype(B)
        key_grad = dot(ds[k0 : k0 + CH, :], qt[...], NT)
        value_grad = dot(pt[...], do2[...], NN)
        gbuf[:, :LAT] = key_grad[:, :LAT] + value_grad
        gbuf[:, LAT:] = key_grad[:, LAT:]
        i = 2 * t + m
        psnd[i] = gbuf[pl.ds(pl.multiple_of((1 - c) * QTR, 32), QTR), :].astype(B)
        gown[i] = gbuf[pl.ds(pl.multiple_of(c * QTR, 32), QTR), :]
        pair(i).start()

    chunk(0, 0)
    chunk(0, 1)
    for i in range(2):
        send_lat[i].wait_recv()
        fwd_lat[i].start()
    for i in range(2):
        pair(i).wait_recv()
        gown[i] = gown[i] + prcv[i].astype(F)
    for i in range(2):
        fwd_lat[i].wait_recv()
    lr[BLOCK:, :] = lt[:, BLOCK:].T
    chunk(1, 0)
    chunk(1, 1)

    def back(m):
        return remote(xs.at[m], xr.at[m], 8 + m, 8 + m, prv, head)

    for m in range(2):
        pair(2 + m).wait_recv()
        xs[m] = (gown[2 + m] + prcv[2 + m].astype(F)).astype(B)
        back(m).start()

    for g in range(4):
        dq = dot(lt[...], ds[:, g * 256 : (g + 1) * 256], NN).astype(B)
        dqb[2 * g] = dq[:, :PACKET]
        dqb[2 * g + 1] = dq[:, PACKET:]
    dq_store = pltpu.make_async_copy(dqb, dq_hbm, lsem.at[10])
    dq_store.start()

    slot = z // 2
    hx = jnp.where((z == 1) | (z == 2), 0, 1)

    def owner_send(k):
        step = jnp.where(slot == k, 1, 3)
        return remote(osb.at[pl.ds(k * HALF, HALF)], mrb.at[slot], 10 + k, 10 + slot, s, chip(z + step))

    def mid_send(buf, dst, n, to):
        step = jnp.where(hx == to, 3, 1)
        return remote(buf.at[to], dst.at[hx], n + to, n + hx, s, chip(z + step))

    for m in range(2):
        back(m).wait_recv()
        p0 = gown[m]
        p1 = xr[m].astype(F)
        sab[0] = p0 * (1.0 - w0) + p1 * (1.0 - w1)
        sab[1] = p0 * w0 + p1 * w1

        @pl.when(lax.rem(z, 2) == m)
        def _():
            acc[...] = sab[slot]
            osb[...] = sab[1 - slot].astype(B)
            for k in range(2):
                owner_send(k).start()

        @pl.when(lax.rem(z, 2) != m)
        def _():
            for b in range(2):
                esb[b] = sab[b, pl.ds(pl.multiple_of((1 - hx) * HALF, 16), HALF), :].astype(B)
                mid_send(esb, early, 12, b).start()
                lsb[b] = sab[b, pl.ds(pl.multiple_of(hx * HALF, 16), HALF), :].astype(B)

    for b in range(2):
        rsem_wait = remote(osb.at[pl.ds(b * HALF, HALF)], mrb.at[1 - b], 10 + b, 11 - b, s, chip(z + 1))
        rsem_wait.wait_recv()
        lsb[b] = (lsb[b].astype(F) + mrb[1 - b].astype(F)).astype(B)
        mid_send(lsb, late, 14, b).start()
    for k in range(2):
        remote(esb.at[k], early.at[k], 12 + k, 12 + k, s, chip(z + 1)).wait_recv()
    for k in range(2):
        remote(lsb.at[k], late.at[k], 14 + k, 14 + k, s, chip(z + 1)).wait_recv()
    out[:HALF, :] = (acc[:HALF, :] + late[0].astype(F) + early[1].astype(F)).astype(B)
    out[HALF:, :] = (acc[HALF:, :] + late[1].astype(F) + early[0].astype(F)).astype(B)

    for copy in send_lat + fwd_lat + [pair(i) for i in range(4)] + [back(m) for m in range(2)]:
        copy.wait_send()
    for k in range(2):
        owner_send(k).wait_send()
        mid_send(esb, early, 12, k).wait_send()
        mid_send(lsb, late, 14, k).wait_send()
    dq_store.wait()


def solution(mesh):
    shards = mesh.shape["seq"]

    def local(queries, out_grad, latents, log_norm, out_delta, plan):
        any_spec = pl.BlockSpec(memory_space=pl.ANY)
        vmem = pl.BlockSpec(memory_space=pltpu.VMEM)
        dq, latent_out = pl.pallas_call(
            lambda *refs: kernel(shards, *refs),
            out_shape=(
                jax.ShapeDtypeStruct((8, KW, PACKET), B),
                jax.ShapeDtypeStruct((QTR, KW), B),
            ),
            in_specs=[pl.BlockSpec(memory_space=pltpu.SMEM), vmem, vmem, any_spec, any_spec, any_spec],
            out_specs=(any_spec, vmem),
            scratch_shapes=[
                pltpu.VMEM((KW, 8 * PACKET), B),
                pltpu.VMEM((PACKET, 8, LAT), B),
                pltpu.VMEM((4, 8 * PACKET, 128), F),
                pltpu.VMEM((8 * PACKET, LAT), B),
                pltpu.VMEM((KW, SHARD), B),
                pltpu.VMEM((KW, SHARD), B),
                pltpu.VMEM((SHARD, KW), B),
                pltpu.VMEM((KW // 2, BLOCK), B),
                pltpu.VMEM((SHARD, 8 * PACKET), B),
                pltpu.VMEM((CH, 8 * PACKET), B),
                pltpu.VMEM((CH, KW), F),
                pltpu.VMEM((4, QTR, KW), F),
                pltpu.VMEM((4, QTR, KW), B),
                pltpu.VMEM((4, QTR, KW), B),
                pltpu.VMEM((2, QTR, KW), B),
                pltpu.VMEM((2, QTR, KW), B),
                pltpu.VMEM((QTR, KW), F),
                pltpu.VMEM((QTR, KW), B),
                pltpu.VMEM((2, QTR, KW), F),
                pltpu.VMEM((2, HALF, KW), B),
                pltpu.VMEM((2, HALF, KW), B),
                pltpu.VMEM((2, HALF, KW), B),
                pltpu.VMEM((2, HALF, KW), B),
                pltpu.VMEM((2, HALF, KW), B),
                pltpu.VMEM((8, KW, PACKET), B),
                pltpu.SemaphoreType.DMA((11,)),
                pltpu.SemaphoreType.DMA((16,)),
                pltpu.SemaphoreType.DMA((16,)),
            ],
            compiler_params=pltpu.CompilerParams(
                collective_id=0, has_side_effects=True, vmem_limit_bytes=60 << 20
            ),
            name="mla_bwd",
        )(plan, log_norm.T, out_delta.T, queries.transpose(1, 2, 0), out_grad, latents.T)
        return dq.transpose(2, 0, 1), latent_out

    return jax.shard_map(
        local,
        mesh=mesh,
        in_specs=(
            P("seq", "head", None),
            P("seq", "head", None),
            P("seq", None),
            P("seq", "head"),
            P("seq", "head"),
            P("seq", None),
        ),
        out_specs=(P("seq", "head", None), P(("seq", "head"), None)),
        check_vma=False,
    )
```

```python
import jax
import jax.numpy as jnp
from jax import lax
from jax.experimental import pallas as pl
from jax.experimental.pallas import tpu as pltpu
from jax.sharding import PartitionSpec as P

LAT = 512
KW = 576
PACKET = 128
BLOCK = 384
SHARD = 768
CH = BLOCK // 2
QTR = BLOCK // 4
HALF = QTR // 2
F = jnp.float32
B = jnp.bfloat16
MESH = pl.DeviceIdType.MESH
NT = (((1,), (1,)), ((), ()))
NN = (((1,), (0,)), ((), ()))


def dot(a, b, dims):
    return lax.dot_general(a, b, dims, preferred_element_type=F)


def kernel(
    shards, plan, nrm, dlt, q_hbm, do_hbm, lat_hbm, dq_hbm, out,
    qt, dob, do32, do2, own, lt, lr, snd, ds, pt, gbuf, gown, psnd, prcv,
    xs, xr, osb, esb, lsb, mrb, early, late, dqb, lsem, ssem, rsem,
):
    s = lax.axis_index("seq")
    head = lax.axis_index("head")
    z = head // 2
    c = head % 2
    nxt = lax.rem(s + 1, shards)
    prv = lax.rem(s + shards - 1, shards)
    mate = 2 * z + 1 - c

    def chip(zz):
        return 2 * lax.rem(zz + 4, 4) + c

    def remote(src, dst, i, j, seq, hd):
        return pltpu.make_async_remote_copy(
            src_ref=src, dst_ref=dst, send_sem=ssem.at[i], recv_sem=rsem.at[j],
            device_id=(seq, hd), device_id_type=MESH,
        )

    loads = [pltpu.make_async_copy(lat_hbm, own, lsem.at[0]), pltpu.make_async_copy(do_hbm, dob, lsem.at[1])]
    for h in range(8):
        loads.append(pltpu.make_async_copy(q_hbm.at[h], qt.at[:, h * PACKET : (h + 1) * PACKET], lsem.at[2 + h]))
    for load in loads:
        load.start()
    barrier = pltpu.get_barrier_semaphore()
    for there in ((s, mate), (s, chip(z + 1)), (s, chip(z - 1))):
        pl.semaphore_signal(barrier, inc=1, device_id=there, device_id_type=MESH)
    first = s == 0
    last = s == shards - 1

    @pl.when(jnp.logical_not(last))
    def _():
        pl.semaphore_signal(barrier, inc=1, device_id=(nxt, head), device_id_type=MESH)

    @pl.when(jnp.logical_not(first))
    def _():
        pl.semaphore_signal(barrier, inc=1, device_id=(prv, head), device_id_type=MESH)

    loads[0].wait()
    rows = pl.ds(pl.multiple_of(c * (KW // 2), 32), KW // 2)
    b0 = plan[0, 0]
    b1 = plan[0, 1]
    w0 = b0.astype(F)
    w1 = b1.astype(F)

    def pick(w, x0, x1):
        return x0.astype(F) * (1.0 - w) + x1.astype(F) * w

    snd[...] = pick(w1, own[rows, :BLOCK], own[rows, BLOCK:]).astype(B)
    lt[:, :BLOCK] = pick(w0, own[:, :BLOCK], own[:, BLOCK:]).astype(B)
    pl.semaphore_wait(barrier, 5 - first.astype(jnp.int32) - last.astype(jnp.int32))
    spans = ((0, 256), (256, 128))
    send_lat = [
        remote(snd.at[:, pl.ds(a, w)], lt.at[rows, pl.ds(BLOCK + a, w)], i, i, nxt, head)
        for i, (a, w) in enumerate(spans)
    ]
    fwd_lat = [
        remote(lt.at[rows, pl.ds(BLOCK + a, w)], lt.at[rows, pl.ds(BLOCK + a, w)], 2 + i, 2 + i, s, mate)
        for i, (a, w) in enumerate(spans)
    ]
    @pl.when(jnp.logical_not(last))
    def _():
        for copy in send_lat:
            copy.start()

    lr[:BLOCK, :] = lt[:, :BLOCK].T
    loads[1].wait()
    for i in range(4):
        do32[i] = dob[:, :, i * 128 : (i + 1) * 128].astype(F).reshape(8 * PACKET, 128)
    for h in range(8):
        for i in range(4):
            do2[h * PACKET : (h + 1) * PACKET, i * 128 : (i + 1) * 128] = do32[i, pl.ds(h, PACKET, stride=8), :].astype(B)
    for load in loads[2:]:
        load.wait()

    def pair(i):
        return remote(psnd.at[i], prcv.at[i], 4 + i, 4 + i, s, mate)

    def chunk(t, m, between=None):
        k0 = t * BLOCK + m * CH
        k = lr[k0 : k0 + CH, :]
        if t == 0 and m == 1:
            key = lax.broadcasted_iota(jnp.int32, (CH, PACKET), 0) + CH
            query = lax.broadcasted_iota(jnp.int32, (CH, PACKET), 1) + (SHARD - PACKET - b0 * BLOCK)
            seen = key <= query
        for g in range(4):
            cols = slice(g * 256, (g + 1) * 256)
            score = dot(k, qt[:, cols], NN)
            grad = dot(k[:, :LAT], do2[cols, :], NT)
            for i in range(2):
                h = 2 * g + i
                part = slice(i * PACKET, (i + 1) * PACKET)
                to = slice(h * PACKET, (h + 1) * PACKET)
                norm = nrm[h : h + 1, :].astype(F)
                prob = jnp.exp(score[:, part] - norm)
                if t == 0 and m == 1:
                    prob = jnp.where(seen, prob, 0.0)
                ds[k0 : k0 + CH, to] = (prob * (grad[:, part] - dlt[h : h + 1, :].astype(F))).astype(B)
                pt[:, to] = prob.astype(B)
        if between is not None:
            between()
        key_grad = dot(ds[k0 : k0 + CH, :], qt[...], NT)
        value_grad = dot(pt[...], do2[...], NN)
        gbuf[:, :LAT] = key_grad[:, :LAT] + value_grad
        gbuf[:, LAT:] = key_grad[:, LAT:]
        i = 2 * t + m
        psnd[i] = gbuf[pl.ds(pl.multiple_of((1 - c) * QTR, 32), QTR), :].astype(B)
        gown[i] = gbuf[pl.ds(pl.multiple_of(c * QTR, 32), QTR), :]
        pair(i).start()

    chunk(0, 0)
    chunk(0, 1)
    slot = z // 2
    hx = jnp.where((z == 1) | (z == 2), 0, 1)
    half = pl.ds(pl.multiple_of(hx * HALF, 16), HALF)
    rest = pl.ds(pl.multiple_of((1 - hx) * HALF, 16), HALF)
    mo = lax.rem(z, 2)
    mm = 1 - mo

    def owner_send(t, k):
        step = jnp.where(slot == k, 1, 3)
        return remote(osb.at[t, pl.ds(k * HALF, HALF)], mrb.at[t, slot], 10 + 2 * t + k, 10 + 2 * t + slot, s, chip(z + step))

    def mid_recv(t, b):
        return remote(osb.at[t, pl.ds(b * HALF, HALF)], mrb.at[t, b], 10 + 2 * t + b, 10 + 2 * t + b, s, chip(z + 1))

    def mid_send(buf, dst, n, to):
        step = jnp.where(hx == to, 3, 1)
        return remote(buf.at[to], dst.at[hx], n + to, n + hx, s, chip(z + step))

    def owner_recv(buf, dst, n, k):
        return remote(buf.at[k], dst.at[k], n + k, n + k, s, chip(z + 1))

    def back(k):
        return remote(xs.at[k], xr.at[k], 8 + k, 8 + k, prv, head)

    def stage(t):
        osb[t] = gown[2 * t + mo].astype(B)
        for k in range(2):
            owner_send(t, k).start()

    def middle(t):
        for b in range(2):
            mid_recv(t, b).wait_recv()
        return gown[2 * t + mm, half, :] + mrb[t, 0].astype(F) + mrb[t, 1].astype(F)

    @pl.when(first)
    def _():
        lt[:, BLOCK:] = jnp.zeros((KW, BLOCK), B)
        ds[BLOCK:, :] = jnp.zeros((BLOCK, 8 * PACKET), B)

    @pl.when(jnp.logical_not(first))
    def _():
        send_lat[0].wait_recv()
        fwd_lat[0].start()

    for i in range(2):
        pair(i).wait_recv()
        gown[i] = gown[i] + prcv[i].astype(F)
    stage(0)

    @pl.when(jnp.logical_not(first))
    def _():
        def between():
            send_lat[1].wait_recv()
            fwd_lat[1].start()

        fwd_lat[0].wait_recv()
        lr[BLOCK : BLOCK + 256, :] = lt[:, BLOCK : BLOCK + 256].T
        chunk(1, 0, between)
        fwd_lat[1].wait_recv()
        lr[BLOCK + 256 :, :] = lt[:, BLOCK + 256 :].T
        chunk(1, 1)
        for m in range(2):
            pair(2 + m).wait_recv()
            gown[2 + m] = gown[2 + m] + prcv[2 + m].astype(F)

            @pl.when(mo == m)
            def _():
                stage(1)

            @pl.when(mo != m)
            def _():
                xs[0] = gown[2 + m, rest, :].astype(B)
                back(0).start()

    @pl.when(last)
    def _():
        xr[...] = jnp.zeros_like(xr)

    for g in range(4):
        dq = dot(lt[...], ds[:, g * 256 : (g + 1) * 256], NN).astype(B)
        dqb[2 * g] = dq[:, :PACKET]
        dqb[2 * g + 1] = dq[:, PACKET:]
    dq_store = pltpu.make_async_copy(dqb, dq_hbm, lsem.at[10])
    dq_store.start()

    def forward(p0, k, buf, dst, n):
        @pl.when(jnp.logical_not(last))
        def _():
            back(k).wait_recv()

        p1 = xr[k].astype(F)
        buf[0] = (p0 * (1.0 - w0) + p1 * (1.0 - w1)).astype(B)
        buf[1] = (p0 * w0 + p1 * w1).astype(B)
        for b in range(2):
            mid_send(buf, dst, n, b).start()

    forward(gown[mm, rest, :], 0, esb, early, 14)

    @pl.when(jnp.logical_not(first))
    def _():
        xs[1] = middle(1).astype(B)
        back(1).start()

    forward(middle(0), 1, lsb, late, 16)
    for k in range(2):
        owner_recv(esb, early, 14, k).wait_recv()
    for k in range(2):
        owner_recv(lsb, late, 16, k).wait_recv()
    out[:HALF, :] = (late[0].astype(F) + early[1].astype(F)).astype(B)
    out[HALF:, :] = (late[1].astype(F) + early[0].astype(F)).astype(B)

    @pl.when(jnp.logical_not(last))
    def _():
        for copy in send_lat:
            copy.wait_send()

    @pl.when(jnp.logical_not(first))
    def _():
        for copy in fwd_lat + [pair(2), pair(3), back(0), back(1), owner_send(1, 0), owner_send(1, 1)]:
            copy.wait_send()

    for i in range(2):
        pair(i).wait_send()
    for k in range(2):
        owner_send(0, k).wait_send()
        mid_send(esb, early, 14, k).wait_send()
        mid_send(lsb, late, 16, k).wait_send()
    dq_store.wait()


def solution(mesh):
    shards = mesh.shape["seq"]

    def local(queries, out_grad, latents, log_norm, out_delta, plan):
        any_spec = pl.BlockSpec(memory_space=pl.ANY)
        vmem = pl.BlockSpec(memory_space=pltpu.VMEM)
        dq, latent_out = pl.pallas_call(
            lambda *refs: kernel(shards, *refs),
            out_shape=(
                jax.ShapeDtypeStruct((8, KW, PACKET), B),
                jax.ShapeDtypeStruct((QTR, KW), B),
            ),
            in_specs=[pl.BlockSpec(memory_space=pltpu.SMEM), vmem, vmem, any_spec, any_spec, any_spec],
            out_specs=(any_spec, vmem),
            scratch_shapes=[
                pltpu.VMEM((KW, 8 * PACKET), B),
                pltpu.VMEM((PACKET, 8, LAT), B),
                pltpu.VMEM((4, 8 * PACKET, 128), F),
                pltpu.VMEM((8 * PACKET, LAT), B),
                pltpu.VMEM((KW, SHARD), B),
                pltpu.VMEM((KW, SHARD), B),
                pltpu.VMEM((SHARD, KW), B),
                pltpu.VMEM((KW // 2, BLOCK), B),
                pltpu.VMEM((SHARD, 8 * PACKET), B),
                pltpu.VMEM((CH, 8 * PACKET), B),
                pltpu.VMEM((CH, KW), F),
                pltpu.VMEM((4, QTR, KW), F),
                pltpu.VMEM((4, QTR, KW), B),
                pltpu.VMEM((4, QTR, KW), B),
                pltpu.VMEM((2, HALF, KW), B),
                pltpu.VMEM((2, HALF, KW), B),
                pltpu.VMEM((2, QTR, KW), B),
                pltpu.VMEM((2, HALF, KW), B),
                pltpu.VMEM((2, HALF, KW), B),
                pltpu.VMEM((2, 2, HALF, KW), B),
                pltpu.VMEM((2, HALF, KW), B),
                pltpu.VMEM((2, HALF, KW), B),
                pltpu.VMEM((8, KW, PACKET), B),
                pltpu.SemaphoreType.DMA((11,)),
                pltpu.SemaphoreType.DMA((18,)),
                pltpu.SemaphoreType.DMA((18,)),
            ],
            compiler_params=pltpu.CompilerParams(
                collective_id=0, has_side_effects=True, vmem_limit_bytes=60 << 20
            ),
            name="mla_bwd",
        )(plan, log_norm.T, out_delta.T, queries.transpose(1, 2, 0), out_grad, latents.T)
        return dq.transpose(2, 0, 1), latent_out

    return jax.shard_map(
        local,
        mesh=mesh,
        in_specs=(
            P("seq", "head", None),
            P("seq", "head", None),
            P("seq", None),
            P("seq", "head"),
            P("seq", "head"),
            P("seq", None),
        ),
        out_specs=(P("seq", "head", None), P(("seq", "head"), None)),
        check_vma=False,
    )
```

```python
import jax
import jax.numpy as jnp
from jax import lax
from jax.experimental import pallas as pl
from jax.experimental.pallas import tpu as pltpu
from jax.sharding import PartitionSpec as P

LAT = 512
KW = 576
PACKET = 128
BLOCK = 384
SHARD = 768
CH = BLOCK // 2
QTR = BLOCK // 4
HALF = QTR // 2
F = jnp.float32
B = jnp.bfloat16
MESH = pl.DeviceIdType.MESH
NT = (((1,), (1,)), ((), ()))
NN = (((1,), (0,)), ((), ()))


def dot(a, b, dims):
    return lax.dot_general(a, b, dims, preferred_element_type=F)


def kernel(
    shards, plan, nrm, dlt, q_hbm, do_hbm, lat_hbm, dq_hbm, out,
    qt, dob, do2, own, lt, lr, snd, ds, pt, gbuf, gown, psnd, prcv,
    dqb, lsem, ssem, rsem, *flat,
):
    bufs = list(zip(flat[::2], flat[1::2]))
    s = lax.axis_index("seq")
    head = lax.axis_index("head")
    z = head // 2
    c = head % 2
    nxt = lax.rem(s + 1, shards)
    prv = lax.rem(s + shards - 1, shards)
    mate = 2 * z + 1 - c

    def chip(zz):
        return 2 * lax.rem(zz + 4, 4) + c

    def remote(src, dst, i, j, seq, hd):
        return pltpu.make_async_remote_copy(
            src_ref=src, dst_ref=dst, send_sem=ssem.at[i], recv_sem=rsem.at[j],
            device_id=(seq, hd), device_id_type=MESH,
        )

    loads = [pltpu.make_async_copy(lat_hbm, own, lsem.at[0]), pltpu.make_async_copy(do_hbm, dob, lsem.at[1])]
    for h in range(8):
        loads.append(pltpu.make_async_copy(q_hbm.at[h], qt.at[:, h * PACKET : (h + 1) * PACKET], lsem.at[2 + h]))
    for load in loads:
        load.start()
    barrier = pltpu.get_barrier_semaphore()
    for there in ((s, mate), (s, chip(z + 1)), (s, chip(z - 1))):
        pl.semaphore_signal(barrier, inc=1, device_id=there, device_id_type=MESH)
    first = s == 0
    last = s == shards - 1

    @pl.when(jnp.logical_not(last))
    def _():
        pl.semaphore_signal(barrier, inc=1, device_id=(nxt, head), device_id_type=MESH)

    @pl.when(jnp.logical_not(first))
    def _():
        pl.semaphore_signal(barrier, inc=1, device_id=(prv, head), device_id_type=MESH)

    loads[0].wait()
    rows = pl.ds(pl.multiple_of(c * (KW // 2), 32), KW // 2)
    b0 = plan[0, 0]
    b1 = plan[0, 1]
    w0 = b0.astype(F)
    w1 = b1.astype(F)

    def pick(w, x0, x1):
        return x0 * (1.0 - w).astype(B) + x1 * w.astype(B)

    snd[...] = pick(w1, own[rows, :BLOCK], own[rows, BLOCK:])
    pl.semaphore_wait(barrier, 5 - first.astype(jnp.int32) - last.astype(jnp.int32))
    spans = ((0, 256), (256, 128))
    send_lat = [
        remote(snd.at[:, pl.ds(a, w)], lt.at[rows, pl.ds(BLOCK + a, w)], i, i, nxt, head)
        for i, (a, w) in enumerate(spans)
    ]
    fwd_lat = [
        remote(lt.at[rows, pl.ds(BLOCK + a, w)], lt.at[rows, pl.ds(BLOCK + a, w)], 2 + i, 2 + i, s, mate)
        for i, (a, w) in enumerate(spans)
    ]
    @pl.when(jnp.logical_not(last))
    def _():
        for copy in send_lat:
            copy.start()

    lt[:, :BLOCK] = pick(w0, own[:, :BLOCK], own[:, BLOCK:])
    lr[:BLOCK, :] = lt[:, :BLOCK].T
    loads[1].wait()
    do2[...] = jnp.swapaxes(dob[...], 0, 1).reshape(8 * PACKET, LAT)
    for load in loads[2:]:
        load.wait()

    def pair(i):
        return remote(psnd.at[i], prcv.at[i], 4 + i, 4 + i, s, mate)

    def chunk(t, m, between=None):
        k0 = t * BLOCK + m * CH
        k = lr[k0 : k0 + CH, :]
        if t == 0 and m == 1:
            key = lax.broadcasted_iota(jnp.int32, (CH, PACKET), 0) + CH
            query = lax.broadcasted_iota(jnp.int32, (CH, PACKET), 1) + (SHARD - PACKET - b0 * BLOCK)
            seen = key <= query
        for g in range(4):
            cols = slice(g * 256, (g + 1) * 256)
            score = dot(k, qt[:, cols], NN)
            grad = dot(k[:, :LAT], do2[cols, :], NT)
            for i in range(2):
                h = 2 * g + i
                part = slice(i * PACKET, (i + 1) * PACKET)
                to = slice(h * PACKET, (h + 1) * PACKET)
                norm = nrm[h : h + 1, :].astype(F)
                prob = jnp.exp(score[:, part] - norm)
                if t == 0 and m == 1:
                    prob = jnp.where(seen, prob, 0.0)
                ds[k0 : k0 + CH, to] = (prob * (grad[:, part] - dlt[h : h + 1, :].astype(F))).astype(B)
                pt[:, to] = prob.astype(B)
        if between is not None:
            between()
        key_grad = dot(ds[k0 : k0 + CH, :], qt[...], NT)
        value_grad = dot(pt[...], do2[...], NN)
        gbuf[:, :LAT] = key_grad[:, :LAT] + value_grad
        gbuf[:, LAT:] = key_grad[:, LAT:]
        i = 2 * t + m
        psnd[i] = gbuf[pl.ds(pl.multiple_of((1 - c) * QTR, 32), QTR), :]
        gown[i] = gbuf[pl.ds(pl.multiple_of(c * QTR, 32), QTR), :]
        pair(i).start()

    chunk(0, 0)
    chunk(0, 1)
    slot = z // 2
    hx = jnp.where((z == 1) | (z == 2), 0, 1)
    mo = lax.rem(z, 2)
    mm = 1 - mo
    parts = range(3)
    ours, sent, middles, home, away, first_s, first_r, last_s, last_r = bufs

    def at(buf, idx, p):
        main, tail = buf
        return main.at[idx + (slice(None), pl.ds(256 * p, 256))] if p < 2 else tail.at[idx]

    def get(buf, idx, p):
        main, tail = buf
        return (main[idx + (slice(None), slice(256 * p, 256 * p + 256))] if p < 2 else tail[idx]).astype(F)

    def put(buf, idx, p, value):
        main, tail = buf
        if p < 2:
            main[idx + (slice(None), slice(256 * p, 256 * p + 256))] = value.astype(B)
        else:
            tail[idx] = value.astype(B)

    def toward(k, same):
        return jnp.where(same == k, 1, 3)

    def owner_send(t, k, p):
        n = 14 + 12 * t + 4 * p
        return remote(at(sent, (t, k), p), at(middles, (t, slot), p), n + k, n + slot, s, chip(z + toward(k, slot)))

    def mid_recv(t, b, p):
        n = 14 + 12 * t + 4 * p
        return remote(at(sent, (t, b), p), at(middles, (t, b), p), n + b, n + b, s, chip(z + 1))

    def early_send(to, p):
        n = 38 + 2 * p
        return remote(at(first_s, (to,), p), at(first_r, (hx,), p), n + to, n + hx, s, chip(z - toward(to, hx)))

    def early_recv(k, p):
        n = 38 + 2 * p
        return remote(at(first_s, (k,), p), at(first_r, (k,), p), n + k, n + k, s, chip(z + 1))

    def late_send(to, p):
        n = 44 + 2 * p
        return remote(at(last_s, (to,), p), at(last_r, (hx,), p), n + to, n + hx, s, chip(z - toward(to, hx)))

    def late_recv(k, p):
        n = 44 + 2 * p
        return remote(at(last_s, (k,), p), at(last_r, (k,), p), n + k, n + k, s, chip(z + 1))

    def back(k, p):
        n = 8 + 3 * k + p
        return remote(at(home, (k,), p), at(away, (k,), p), n, n, prv, head)

    def stage(t):
        for p in parts:
            for k in range(2):
                put(sent, (t, k), p, get(ours, (2 * t + mo, k), p))
                owner_send(t, k, p).start()

    def middle(t, p):
        for b in range(2):
            mid_recv(t, b, p).wait_recv()
        return get(ours, (2 * t + mm, hx), p) + get(middles, (t, 0), p) + get(middles, (t, 1), p)

    def settle(i):
        pair(i).wait_recv()
        value = gown[i] + prcv[i]
        for k in range(2):
            ours[0][i, k] = value[k * HALF : (k + 1) * HALF, :LAT]
            a = k * HALF
            ours[1][i, k] = jnp.concatenate([value[a : a + HALF // 2, LAT:], value[a + HALF // 2 : a + HALF, LAT:]], axis=1)

    @pl.when(first)
    def _():
        lt[:, BLOCK:] = jnp.zeros((KW, BLOCK), B)
        ds[BLOCK:, :] = jnp.zeros((BLOCK, 8 * PACKET), B)

    @pl.when(jnp.logical_not(first))
    def _():
        send_lat[0].wait_recv()
        fwd_lat[0].start()

    settle(0)
    settle(1)
    stage(0)

    @pl.when(jnp.logical_not(first))
    def _():
        def between():
            send_lat[1].wait_recv()
            fwd_lat[1].start()

        fwd_lat[0].wait_recv()
        lr[BLOCK : BLOCK + 256, :] = lt[:, BLOCK : BLOCK + 256].T
        chunk(1, 0, between)
        fwd_lat[1].wait_recv()
        lr[BLOCK + 256 :, :] = lt[:, BLOCK + 256 :].T
        chunk(1, 1)
        for m in range(2):
            settle(2 + m)

            @pl.when(mo == m)
            def _():
                stage(1)

            @pl.when(mo != m)
            def _():
                for p in parts:
                    put(home, (0,), p, get(ours, (2 + m, 1 - hx), p))
                    back(0, p).start()

    @pl.when(last)
    def _():
        for ref in away:
            ref[...] = jnp.zeros_like(ref)

    for g in range(4):
        dq = dot(lt[...], ds[:, g * 256 : (g + 1) * 256], NN).astype(B)
        dqb[2 * g] = dq[:, :PACKET]
        dqb[2 * g + 1] = dq[:, PACKET:]
    dq_store = pltpu.make_async_copy(dqb, dq_hbm, lsem.at[10])
    dq_store.start()

    def slots(p0, p1):
        return p0 * (1.0 - w0) + p1 * (1.0 - w1), p0 * w0 + p1 * w1

    def arrived(k, p):
        @pl.when(jnp.logical_not(last))
        def _():
            back(k, p).wait_recv()

    for p in parts:
        arrived(0, p)
        for b, value in enumerate(slots(get(ours, (mm, 1 - hx), p), get(away, (0,), p))):
            put(first_s, (b,), p, value)
            early_send(b, p).start()

    @pl.when(jnp.logical_not(first))
    def _():
        for p in parts:
            put(home, (1,), p, middle(1, p))
            back(1, p).start()

    for p in parts:
        mid0 = middle(0, p)
        arrived(1, p)
        for b, value in enumerate(slots(mid0, get(away, (1,), p))):
            put(last_s, (b,), p, value)
            late_send(b, p).start()
    for p in parts:
        for k in range(2):
            early_recv(k, p).wait_recv()
    for p in parts:
        for k in range(2):
            late_recv(k, p).wait_recv()
            value = get(last_r, (k,), p) + get(first_r, (1 - k,), p)
            if p < 2:
                out[k * HALF : (k + 1) * HALF, 256 * p : 256 * p + 256] = value.astype(B)
            else:
                width = KW - LAT
                out[k * HALF : (k + 1) * HALF, LAT:] = jnp.concatenate([value[:, :width], value[:, width:]], axis=0).astype(B)

    @pl.when(jnp.logical_not(last))
    def _():
        for copy in send_lat:
            copy.wait_send()

    @pl.when(jnp.logical_not(first))
    def _():
        for copy in fwd_lat + [pair(2), pair(3)]:
            copy.wait_send()
        for p in parts:
            for k in range(2):
                back(k, p).wait_send()
                owner_send(1, k, p).wait_send()

    for i in range(2):
        pair(i).wait_send()
    for k in range(2):
        for p in parts:
            early_send(k, p).wait_send()
            owner_send(0, k, p).wait_send()
            late_send(k, p).wait_send()
    dq_store.wait()


def solution(mesh):
    shards = mesh.shape["seq"]

    def local(queries, out_grad, latents, log_norm, out_delta, plan):
        any_spec = pl.BlockSpec(memory_space=pl.ANY)
        vmem = pl.BlockSpec(memory_space=pltpu.VMEM)
        payloads = []
        for lead, kind in (((4, 2), F), ((2, 2), B), ((2, 2), B)) + (((2,), B),) * 6:
            payloads.append(pltpu.VMEM(lead + (HALF, LAT), kind))
            payloads.append(pltpu.VMEM(lead + (HALF // 2, 128), kind))
        dq, latent_out = pl.pallas_call(
            lambda *refs: kernel(shards, *refs),
            out_shape=(
                jax.ShapeDtypeStruct((8, KW, PACKET), B),
                jax.ShapeDtypeStruct((QTR, KW), B),
            ),
            in_specs=[pl.BlockSpec(memory_space=pltpu.SMEM), vmem, vmem, any_spec, any_spec, any_spec],
            out_specs=(any_spec, vmem),
            scratch_shapes=[
                pltpu.VMEM((KW, 8 * PACKET), B),
                pltpu.VMEM((PACKET, 8, LAT), B),
                pltpu.VMEM((8 * PACKET, LAT), B),
                pltpu.VMEM((KW, SHARD), B),
                pltpu.VMEM((KW, SHARD), B),
                pltpu.VMEM((SHARD, KW), B),
                pltpu.VMEM((KW // 2, BLOCK), B),
                pltpu.VMEM((SHARD, 8 * PACKET), B),
                pltpu.VMEM((CH, 8 * PACKET), B),
                pltpu.VMEM((CH, KW), F),
                pltpu.VMEM((4, QTR, KW), F),
                pltpu.VMEM((4, QTR, KW), F),
                pltpu.VMEM((4, QTR, KW), F),
                pltpu.VMEM((8, KW, PACKET), B),
                pltpu.SemaphoreType.DMA((11,)),
                pltpu.SemaphoreType.DMA((50,)),
                pltpu.SemaphoreType.DMA((50,)),
            ]
            + payloads,
            compiler_params=pltpu.CompilerParams(
                collective_id=0, has_side_effects=True, vmem_limit_bytes=60 << 20
            ),
            name="mla_bwd",
        )(plan, log_norm.T, out_delta.T, queries.transpose(1, 2, 0), out_grad, latents.T)

        def put(a_ref, b_ref, c_ref, d_ref, buf, bufc, sem):
            ins = [pltpu.make_async_copy(a_ref.at[h], buf.at[h], sem.at[h]) for h in range(8)]
            ins.append(pltpu.make_async_copy(b_ref, bufc, sem.at[8]))
            outs = [pltpu.make_async_copy(buf.at[h], c_ref.at[h], sem.at[9 + h]) for h in range(8)]
            outs.append(pltpu.make_async_copy(bufc, d_ref, sem.at[17]))
            for i in ins:
                i.start()
            for i, o in zip(ins, outs):
                i.wait()
                o.start()
            for o in outs:
                o.wait()

        dq, latent_out = pl.pallas_call(
            put,
            out_shape=(
                jax.ShapeDtypeStruct((8, KW, PACKET), B),
                jax.ShapeDtypeStruct((QTR, KW), B),
            ),
            in_specs=[any_spec, any_spec],
            out_specs=(any_spec, any_spec),
            scratch_shapes=[
                pltpu.VMEM((8, KW, PACKET), B),
                pltpu.VMEM((QTR, KW), B),
                pltpu.SemaphoreType.DMA((18,)),
            ],
            compiler_params=pltpu.CompilerParams(vmem_limit_bytes=60 << 20),
            name="mla_put",
        )(dq, latent_out)
        return dq.transpose(2, 0, 1), latent_out

    return jax.shard_map(
        local,
        mesh=mesh,
        in_specs=(
            P("seq", "head", None),
            P("seq", "head", None),
            P("seq", None),
            P("seq", "head"),
            P("seq", "head"),
            P("seq", None),
        ),
        out_specs=(P("seq", "head", None), P(("seq", "head"), None)),
        check_vma=False,
    )
```

```python
import jax
import jax.numpy as jnp
from jax import lax
from jax.experimental import pallas as pl
from jax.experimental.pallas import tpu as pltpu
from jax.sharding import PartitionSpec as P

LAT = 512
KW = 576
PACKET = 128
BLOCK = 384
SHARD = 768
CH = BLOCK // 2
QTR = BLOCK // 4
HALF = QTR // 2
F = jnp.float32
B = jnp.bfloat16
MESH = pl.DeviceIdType.MESH
NT = (((1,), (1,)), ((), ()))
NN = (((1,), (0,)), ((), ()))


def dot(a, b, dims):
    return lax.dot_general(a, b, dims, preferred_element_type=F)


def kernel(
    shards, plan, nrm, dlt, q_hbm, do_hbm, lat_hbm, dqb, out,
    qt, dob, do2, own, lt, lr, snd, ds, pt, gbuf, gown, psnd, prcv,
    lsem, ssem, rsem, *flat,
):
    bufs = list(zip(flat[::2], flat[1::2]))
    s = lax.axis_index("seq")
    head = lax.axis_index("head")
    z = head // 2
    c = head % 2
    nxt = lax.rem(s + 1, shards)
    prv = lax.rem(s + shards - 1, shards)
    mate = 2 * z + 1 - c

    def chip(zz):
        return 2 * lax.rem(zz + 4, 4) + c

    def remote(src, dst, i, j, seq, hd):
        return pltpu.make_async_remote_copy(
            src_ref=src, dst_ref=dst, send_sem=ssem.at[i], recv_sem=rsem.at[j],
            device_id=(seq, hd), device_id_type=MESH,
        )

    loads = [pltpu.make_async_copy(lat_hbm, own, lsem.at[0]), pltpu.make_async_copy(do_hbm, dob, lsem.at[1])]
    for h in range(8):
        loads.append(pltpu.make_async_copy(q_hbm.at[h], qt.at[:, h * PACKET : (h + 1) * PACKET], lsem.at[2 + h]))
    for load in loads:
        load.start()
    barrier = pltpu.get_barrier_semaphore()
    for there in ((s, mate), (s, chip(z + 1)), (s, chip(z - 1))):
        pl.semaphore_signal(barrier, inc=1, device_id=there, device_id_type=MESH)
    first = s == 0
    last = s == shards - 1

    @pl.when(jnp.logical_not(last))
    def _():
        pl.semaphore_signal(barrier, inc=1, device_id=(nxt, head), device_id_type=MESH)

    @pl.when(jnp.logical_not(first))
    def _():
        pl.semaphore_signal(barrier, inc=1, device_id=(prv, head), device_id_type=MESH)

    loads[0].wait()
    rows = pl.ds(pl.multiple_of(c * (KW // 2), 32), KW // 2)
    b0 = plan[0, 0]
    b1 = plan[0, 1]
    w0 = b0.astype(F)
    w1 = b1.astype(F)

    def pick(w, x0, x1):
        return x0 * (1.0 - w).astype(B) + x1 * w.astype(B)

    snd[...] = pick(w1, own[rows, :BLOCK], own[rows, BLOCK:])
    pl.semaphore_wait(barrier, 5 - first.astype(jnp.int32) - last.astype(jnp.int32))
    spans = ((0, 256), (256, 128))
    send_lat = [
        remote(snd.at[:, pl.ds(a, w)], lt.at[rows, pl.ds(BLOCK + a, w)], i, i, nxt, head)
        for i, (a, w) in enumerate(spans)
    ]
    fwd_lat = [
        remote(lt.at[rows, pl.ds(BLOCK + a, w)], lt.at[rows, pl.ds(BLOCK + a, w)], 2 + i, 2 + i, s, mate)
        for i, (a, w) in enumerate(spans)
    ]
    @pl.when(jnp.logical_not(last))
    def _():
        for copy in send_lat:
            copy.start()

    lt[:, :BLOCK] = pick(w0, own[:, :BLOCK], own[:, BLOCK:])
    lr[:BLOCK, :] = lt[:, :BLOCK].T
    loads[1].wait()
    do2[...] = jnp.swapaxes(dob[...], 0, 1).reshape(8 * PACKET, LAT)
    for load in loads[2:]:
        load.wait()

    def pair(i):
        return remote(psnd.at[i], prcv.at[i], 4 + i, 4 + i, s, mate)

    def chunk(t, m, between=None):
        k0 = t * BLOCK + m * CH
        k = lr[k0 : k0 + CH, :]
        if t == 0 and m == 1:
            key = lax.broadcasted_iota(jnp.int32, (CH, PACKET), 0) + CH
            query = lax.broadcasted_iota(jnp.int32, (CH, PACKET), 1) + (SHARD - PACKET - b0 * BLOCK)
            seen = key <= query
        for g in range(4):
            cols = slice(g * 256, (g + 1) * 256)
            score = dot(k, qt[:, cols], NN)
            grad = dot(k[:, :LAT], do2[cols, :], NT)
            for i in range(2):
                h = 2 * g + i
                part = slice(i * PACKET, (i + 1) * PACKET)
                to = slice(h * PACKET, (h + 1) * PACKET)
                norm = nrm[h : h + 1, :].astype(F)
                prob = jnp.exp(score[:, part] - norm)
                if t == 0 and m == 1:
                    prob = jnp.where(seen, prob, 0.0)
                ds[k0 : k0 + CH, to] = (prob * (grad[:, part] - dlt[h : h + 1, :].astype(F))).astype(B)
                pt[:, to] = prob.astype(B)
        if between is not None:
            between()
        key_grad = dot(ds[k0 : k0 + CH, :], qt[...], NT)
        value_grad = dot(pt[...], do2[...], NN)
        gbuf[:, :LAT] = key_grad[:, :LAT] + value_grad
        gbuf[:, LAT:] = key_grad[:, LAT:]
        i = 2 * t + m
        psnd[i] = gbuf[pl.ds(pl.multiple_of((1 - c) * QTR, 32), QTR), :]
        gown[i] = gbuf[pl.ds(pl.multiple_of(c * QTR, 32), QTR), :]
        pair(i).start()

    chunk(0, 0)
    chunk(0, 1)
    slot = z // 2
    hx = jnp.where((z == 1) | (z == 2), 0, 1)
    mo = lax.rem(z, 2)
    mm = 1 - mo
    parts = range(3)
    ours, sent, middles, home, away, first_s, first_r, last_s, last_r = bufs

    def at(buf, idx, p):
        main, tail = buf
        return main.at[idx + (slice(None), pl.ds(256 * p, 256))] if p < 2 else tail.at[idx]

    def get(buf, idx, p):
        main, tail = buf
        return (main[idx + (slice(None), slice(256 * p, 256 * p + 256))] if p < 2 else tail[idx]).astype(F)

    def put(buf, idx, p, value):
        main, tail = buf
        if p < 2:
            main[idx + (slice(None), slice(256 * p, 256 * p + 256))] = value.astype(B)
        else:
            tail[idx] = value.astype(B)

    def toward(k, same):
        return jnp.where(same == k, 1, 3)

    def owner_send(t, k, p):
        n = 14 + 12 * t + 4 * p
        return remote(at(sent, (t, k), p), at(middles, (t, slot), p), n + k, n + slot, s, chip(z + toward(k, slot)))

    def mid_recv(t, b, p):
        n = 14 + 12 * t + 4 * p
        return remote(at(sent, (t, b), p), at(middles, (t, b), p), n + b, n + b, s, chip(z + 1))

    def early_send(to, p):
        n = 38 + 2 * p
        return remote(at(first_s, (to,), p), at(first_r, (hx,), p), n + to, n + hx, s, chip(z - toward(to, hx)))

    def early_recv(k, p):
        n = 38 + 2 * p
        return remote(at(first_s, (k,), p), at(first_r, (k,), p), n + k, n + k, s, chip(z + 1))

    def late_send(to, p):
        n = 44 + 2 * p
        return remote(at(last_s, (to,), p), at(last_r, (hx,), p), n + to, n + hx, s, chip(z - toward(to, hx)))

    def late_recv(k, p):
        n = 44 + 2 * p
        return remote(at(last_s, (k,), p), at(last_r, (k,), p), n + k, n + k, s, chip(z + 1))

    def back(k, p):
        n = 8 + 3 * k + p
        return remote(at(home, (k,), p), at(away, (k,), p), n, n, prv, head)

    def stage(t):
        for p in parts:
            for k in range(2):
                put(sent, (t, k), p, get(ours, (2 * t + mo, k), p))
                owner_send(t, k, p).start()

    def middle(t, p):
        for b in range(2):
            mid_recv(t, b, p).wait_recv()
        return get(ours, (2 * t + mm, hx), p) + get(middles, (t, 0), p) + get(middles, (t, 1), p)

    def settle(i):
        pair(i).wait_recv()
        value = gown[i] + prcv[i]
        for k in range(2):
            ours[0][i, k] = value[k * HALF : (k + 1) * HALF, :LAT]
            a = k * HALF
            ours[1][i, k] = jnp.concatenate([value[a : a + HALF // 2, LAT:], value[a + HALF // 2 : a + HALF, LAT:]], axis=1)

    @pl.when(first)
    def _():
        lt[:, BLOCK:] = jnp.zeros((KW, BLOCK), B)
        ds[BLOCK:, :] = jnp.zeros((BLOCK, 8 * PACKET), B)

    @pl.when(jnp.logical_not(first))
    def _():
        send_lat[0].wait_recv()
        fwd_lat[0].start()

    settle(0)
    settle(1)
    stage(0)

    @pl.when(jnp.logical_not(first))
    def _():
        def between():
            send_lat[1].wait_recv()
            fwd_lat[1].start()

        fwd_lat[0].wait_recv()
        lr[BLOCK : BLOCK + 256, :] = lt[:, BLOCK : BLOCK + 256].T
        chunk(1, 0, between)
        fwd_lat[1].wait_recv()
        lr[BLOCK + 256 :, :] = lt[:, BLOCK + 256 :].T
        chunk(1, 1)
        for m in range(2):
            settle(2 + m)

            @pl.when(mo == m)
            def _():
                stage(1)

            @pl.when(mo != m)
            def _():
                for p in parts:
                    put(home, (0,), p, get(ours, (2 + m, 1 - hx), p))
                    back(0, p).start()

    @pl.when(last)
    def _():
        for ref in away:
            ref[...] = jnp.zeros_like(ref)

    for g in range(4):
        dq = dot(lt[...], ds[:, g * 256 : (g + 1) * 256], NN).astype(B)
        dqb[2 * g] = dq[:, :PACKET]
        dqb[2 * g + 1] = dq[:, PACKET:]

    def slots(p0, p1):
        return p0 * (1.0 - w0) + p1 * (1.0 - w1), p0 * w0 + p1 * w1

    def arrived(k, p):
        @pl.when(jnp.logical_not(last))
        def _():
            back(k, p).wait_recv()

    for p in parts:
        arrived(0, p)
        for b, value in enumerate(slots(get(ours, (mm, 1 - hx), p), get(away, (0,), p))):
            put(first_s, (b,), p, value)
            early_send(b, p).start()

    @pl.when(jnp.logical_not(first))
    def _():
        for p in parts:
            put(home, (1,), p, middle(1, p))
            back(1, p).start()

    for p in parts:
        mid0 = middle(0, p)
        arrived(1, p)
        for b, value in enumerate(slots(mid0, get(away, (1,), p))):
            put(last_s, (b,), p, value)
            late_send(b, p).start()
    for p in parts:
        for k in range(2):
            early_recv(k, p).wait_recv()
    for p in parts:
        for k in range(2):
            late_recv(k, p).wait_recv()
            value = get(last_r, (k,), p) + get(first_r, (1 - k,), p)
            if p < 2:
                out[k * HALF : (k + 1) * HALF, 256 * p : 256 * p + 256] = value.astype(B)
            else:
                width = KW - LAT
                out[k * HALF : (k + 1) * HALF, LAT:] = jnp.concatenate([value[:, :width], value[:, width:]], axis=0).astype(B)

    @pl.when(jnp.logical_not(last))
    def _():
        for copy in send_lat:
            copy.wait_send()

    @pl.when(jnp.logical_not(first))
    def _():
        for copy in fwd_lat + [pair(2), pair(3)]:
            copy.wait_send()
        for p in parts:
            for k in range(2):
                back(k, p).wait_send()
                owner_send(1, k, p).wait_send()

    for i in range(2):
        pair(i).wait_send()
    for k in range(2):
        for p in parts:
            early_send(k, p).wait_send()
            owner_send(0, k, p).wait_send()
            late_send(k, p).wait_send()


def solution(mesh):
    shards = mesh.shape["seq"]

    def local(queries, out_grad, latents, log_norm, out_delta, plan):
        any_spec = pl.BlockSpec(memory_space=pl.ANY)
        vmem = pl.BlockSpec(memory_space=pltpu.VMEM)
        payloads = []
        for lead, kind in (((4, 2), F), ((2, 2), B), ((2, 2), B)) + (((2,), B),) * 6:
            payloads.append(pltpu.VMEM(lead + (HALF, LAT), kind))
            payloads.append(pltpu.VMEM(lead + (HALF // 2, 128), kind))
        dq, latent_out = pl.pallas_call(
            lambda *refs: kernel(shards, *refs),
            out_shape=(
                pltpu.VMEM((8, KW, PACKET), B),
                pltpu.VMEM((QTR, KW), B),
            ),
            in_specs=[pl.BlockSpec(memory_space=pltpu.SMEM), vmem, vmem, any_spec, any_spec, any_spec],
            out_specs=(vmem, vmem),
            scratch_shapes=[
                pltpu.VMEM((KW, 8 * PACKET), B),
                pltpu.VMEM((PACKET, 8, LAT), B),
                pltpu.VMEM((8 * PACKET, LAT), B),
                pltpu.VMEM((KW, SHARD), B),
                pltpu.VMEM((KW, SHARD), B),
                pltpu.VMEM((SHARD, KW), B),
                pltpu.VMEM((KW // 2, BLOCK), B),
                pltpu.VMEM((SHARD, 8 * PACKET), B),
                pltpu.VMEM((CH, 8 * PACKET), B),
                pltpu.VMEM((CH, KW), F),
                pltpu.VMEM((4, QTR, KW), F),
                pltpu.VMEM((4, QTR, KW), F),
                pltpu.VMEM((4, QTR, KW), F),
                pltpu.SemaphoreType.DMA((10,)),
                pltpu.SemaphoreType.DMA((50,)),
                pltpu.SemaphoreType.DMA((50,)),
            ]
            + payloads,
            compiler_params=pltpu.CompilerParams(
                collective_id=0, has_side_effects=True, vmem_limit_bytes=60 << 20
            ),
            name="mla_bwd",
        )(plan, log_norm.T, out_delta.T, queries.transpose(1, 2, 0), out_grad, latents.T)

        def put(a_ref, b_ref, c_ref, d_ref, sem):
            outs = [pltpu.make_async_copy(a_ref.at[h], c_ref.at[h], sem.at[h]) for h in range(8)]
            outs.append(pltpu.make_async_copy(b_ref, d_ref, sem.at[8]))
            for o in outs:
                o.start()
            for o in outs:
                o.wait()

        dq, latent_out = pl.pallas_call(
            put,
            out_shape=(
                jax.ShapeDtypeStruct((8, KW, PACKET), B),
                jax.ShapeDtypeStruct((QTR, KW), B),
            ),
            in_specs=[vmem, vmem],
            out_specs=(any_spec, any_spec),
            scratch_shapes=[
                pltpu.SemaphoreType.DMA((9,)),
            ],
            compiler_params=pltpu.CompilerParams(vmem_limit_bytes=4 << 20),
            name="mla_put",
        )(dq, latent_out)
        return dq.transpose(2, 0, 1), latent_out

    return jax.shard_map(
        local,
        mesh=mesh,
        in_specs=(
            P("seq", "head", None),
            P("seq", "head", None),
            P("seq", None),
            P("seq", "head"),
            P("seq", "head"),
            P("seq", None),
        ),
        out_specs=(P("seq", "head", None), P(("seq", "head"), None)),
        check_vma=False,
    )
```

```python
import jax
import jax.numpy as jnp
from jax import lax
from jax.experimental import pallas as pl
from jax.experimental.pallas import tpu as pltpu
from jax.sharding import PartitionSpec as P

LAT = 512
KW = 576
PACKET = 128
BLOCK = 384
SHARD = 768
CH = BLOCK // 2
QTR = BLOCK // 4
HALF = QTR // 2
F = jnp.float32
B = jnp.bfloat16
MESH = pl.DeviceIdType.MESH
NT = (((1,), (1,)), ((), ()))
NN = (((1,), (0,)), ((), ()))


def dot(a, b, dims):
    return lax.dot_general(a, b, dims, preferred_element_type=F)


def kernel(
    shards, plan, nrm, dlt, q_hbm, do_hbm, lat_hbm, dqb, out,
    qt, dob, do2, own, lt, lr, snd, ds, pt, gbuf, gown, psnd, prcv,
    lsem, ssem, rsem, *flat,
):
    bufs = list(zip(flat[::2], flat[1::2]))
    s = lax.axis_index("seq")
    head = lax.axis_index("head")
    z = head // 2
    c = head % 2
    nxt = lax.rem(s + 1, shards)
    prv = lax.rem(s + shards - 1, shards)
    mate = 2 * z + 1 - c

    def chip(zz):
        return 2 * lax.rem(zz + 4, 4) + c

    def remote(src, dst, i, j, seq, hd):
        return pltpu.make_async_remote_copy(
            src_ref=src, dst_ref=dst, send_sem=ssem.at[i], recv_sem=rsem.at[j],
            device_id=(seq, hd), device_id_type=MESH,
        )

    loads = [pltpu.make_async_copy(lat_hbm, own, lsem.at[0]), pltpu.make_async_copy(do_hbm, dob, lsem.at[1])]
    for h in range(8):
        loads.append(pltpu.make_async_copy(q_hbm.at[h], qt.at[:, h * PACKET : (h + 1) * PACKET], lsem.at[2 + h]))
    for load in loads:
        load.start()
    barrier = pltpu.get_barrier_semaphore()
    for there in ((s, mate), (s, chip(z + 1)), (s, chip(z - 1))):
        pl.semaphore_signal(barrier, inc=1, device_id=there, device_id_type=MESH)
    first = s == 0
    last = s == shards - 1

    @pl.when(jnp.logical_not(last))
    def _():
        pl.semaphore_signal(barrier, inc=1, device_id=(nxt, head), device_id_type=MESH)

    @pl.when(jnp.logical_not(first))
    def _():
        pl.semaphore_signal(barrier, inc=1, device_id=(prv, head), device_id_type=MESH)

    loads[0].wait()
    rows = pl.ds(pl.multiple_of(c * (KW // 2), 32), KW // 2)
    b0 = plan[0, 0]
    b1 = plan[0, 1]
    w0 = b0.astype(F)
    w1 = b1.astype(F)

    def pick(w, x0, x1):
        return x0 * (1.0 - w).astype(B) + x1 * w.astype(B)

    snd[...] = pick(w1, own[rows, :BLOCK], own[rows, BLOCK:])
    pl.semaphore_wait(barrier, 5 - first.astype(jnp.int32) - last.astype(jnp.int32))
    mo = lax.rem(z, 2)
    mm = 1 - mo
    spans = ((pl.multiple_of(128 * mo, 128), 256), (pl.multiple_of(256 * mm, 128), 128))
    send_lat = [
        remote(snd.at[:, pl.ds(a, w)], lt.at[rows, pl.ds(pl.multiple_of(BLOCK + a, 128), w)], i, i, nxt, head)
        for i, (a, w) in enumerate(spans)
    ]
    fwd_lat = [
        remote(lt.at[rows, pl.ds(pl.multiple_of(BLOCK + a, 128), w)], lt.at[rows, pl.ds(pl.multiple_of(BLOCK + a, 128), w)], 2 + i, 2 + i, s, mate)
        for i, (a, w) in enumerate(spans)
    ]
    @pl.when(jnp.logical_not(last))
    def _():
        for copy in send_lat:
            copy.start()

    lt[:, :BLOCK] = pick(w0, own[:, :BLOCK], own[:, BLOCK:])
    lr[:BLOCK, :] = lt[:, :BLOCK].T
    loads[1].wait()
    do2[...] = jnp.swapaxes(dob[...], 0, 1).reshape(8 * PACKET, LAT)
    for load in loads[2:]:
        load.wait()

    def pair(i):
        return remote(psnd.at[i], prcv.at[i], 4 + i, 4 + i, s, mate)

    def chunk(t, m, between=None):
        k0 = pl.multiple_of(t * BLOCK + m * CH, 64)
        k = lr[pl.ds(k0, CH), :]
        masked = t == 0 and m == 1
        if masked:
            key = lax.broadcasted_iota(jnp.int32, (CH, PACKET), 0) + CH
            query = lax.broadcasted_iota(jnp.int32, (CH, PACKET), 1) + (SHARD - PACKET - b0 * BLOCK)
            seen = key <= query
        for g in range(4):
            cols = slice(g * 256, (g + 1) * 256)
            score = dot(k, qt[:, cols], NN)
            grad = dot(k[:, :LAT], do2[cols, :], NT)
            for i in range(2):
                h = 2 * g + i
                part = slice(i * PACKET, (i + 1) * PACKET)
                to = slice(h * PACKET, (h + 1) * PACKET)
                norm = nrm[h : h + 1, :].astype(F)
                prob = jnp.exp(score[:, part] - norm)
                if masked:
                    prob = jnp.where(seen, prob, 0.0)
                ds[pl.ds(k0, CH), to] = (prob * (grad[:, part] - dlt[h : h + 1, :].astype(F))).astype(B)
                pt[:, to] = prob.astype(B)
        if between is not None:
            between()
        key_grad = dot(ds[pl.ds(k0, CH), :], qt[...], NT)
        value_grad = dot(pt[...], do2[...], NN)
        gbuf[:, :LAT] = key_grad[:, :LAT] + value_grad
        gbuf[:, LAT:] = key_grad[:, LAT:]
        i = 2 * t + m
        psnd[i] = gbuf[pl.ds(pl.multiple_of((1 - c) * QTR, 32), QTR), :]
        gown[i] = gbuf[pl.ds(pl.multiple_of(c * QTR, 32), QTR), :]
        pair(i).start()

    chunk(0, 0)
    chunk(0, 1)
    slot = z // 2
    hx = jnp.where((z == 1) | (z == 2), 0, 1)
    parts = range(3)
    ours, sent, middles, home, away, first_s, first_r, last_s, last_r = bufs

    def at(buf, idx, p):
        main, tail = buf
        return main.at[idx + (slice(None), pl.ds(256 * p, 256))] if p < 2 else tail.at[idx]

    def get(buf, idx, p):
        main, tail = buf
        return (main[idx + (slice(None), slice(256 * p, 256 * p + 256))] if p < 2 else tail[idx]).astype(F)

    def put(buf, idx, p, value):
        main, tail = buf
        if p < 2:
            main[idx + (slice(None), slice(256 * p, 256 * p + 256))] = value.astype(B)
        else:
            tail[idx] = value.astype(B)

    def toward(k, same):
        return jnp.where(same == k, 1, 3)

    def owner_send(t, k, p):
        n = 14 + 12 * t + 4 * p
        return remote(at(sent, (t, k), p), at(middles, (t, slot), p), n + k, n + slot, s, chip(z + toward(k, slot)))

    def mid_recv(t, b, p):
        n = 14 + 12 * t + 4 * p
        return remote(at(sent, (t, b), p), at(middles, (t, b), p), n + b, n + b, s, chip(z + 1))

    def early_send(to, p):
        n = 38 + 2 * p
        return remote(at(first_s, (to,), p), at(first_r, (hx,), p), n + to, n + hx, s, chip(z - toward(to, hx)))

    def early_recv(k, p):
        n = 38 + 2 * p
        return remote(at(first_s, (k,), p), at(first_r, (k,), p), n + k, n + k, s, chip(z + 1))

    def late_send(to, p):
        n = 44 + 2 * p
        return remote(at(last_s, (to,), p), at(last_r, (hx,), p), n + to, n + hx, s, chip(z - toward(to, hx)))

    def late_recv(k, p):
        n = 44 + 2 * p
        return remote(at(last_s, (k,), p), at(last_r, (k,), p), n + k, n + k, s, chip(z + 1))

    def back(k, p):
        n = 8 + 3 * k + p
        return remote(at(home, (k,), p), at(away, (k,), p), n, n, prv, head)

    def stage(t):
        for p in parts:
            for k in range(2):
                put(sent, (t, k), p, get(ours, (2 * t + mo, k), p))
                owner_send(t, k, p).start()

    def middle(t, p):
        for b in range(2):
            mid_recv(t, b, p).wait_recv()
        return get(ours, (2 * t + mm, hx), p) + get(middles, (t, 0), p) + get(middles, (t, 1), p)

    def settle(i):
        pair(i).wait_recv()
        value = gown[i] + prcv[i]
        for k in range(2):
            ours[0][i, k] = value[k * HALF : (k + 1) * HALF, :LAT]
            a = k * HALF
            ours[1][i, k] = jnp.concatenate([value[a : a + HALF // 2, LAT:], value[a + HALF // 2 : a + HALF, LAT:]], axis=1)

    @pl.when(first)
    def _():
        lt[:, BLOCK:] = jnp.zeros((KW, BLOCK), B)
        ds[BLOCK:, :] = jnp.zeros((BLOCK, 8 * PACKET), B)

    @pl.when(jnp.logical_not(first))
    def _():
        send_lat[0].wait_recv()
        fwd_lat[0].start()

    settle(0)
    settle(1)
    stage(0)

    @pl.when(jnp.logical_not(first))
    def _():
        def between():
            send_lat[1].wait_recv()
            fwd_lat[1].start()

        def own_part():
            settle(2 + mo)
            stage(1)

        def turned(a, w):
            at_a = pl.ds(pl.multiple_of(BLOCK + a, 128), w)
            lr[at_a, :] = lt[:, at_a].T

        fwd_lat[0].wait_recv()
        turned(*spans[0])
        chunk(1, mo, between)
        fwd_lat[1].wait_recv()
        turned(*spans[1])
        chunk(1, mm, own_part)
        settle(2 + mm)
        for p in parts:
            put(home, (0,), p, get(ours, (2 + mm, 1 - hx), p))
            back(0, p).start()

    @pl.when(last)
    def _():
        for ref in away:
            ref[...] = jnp.zeros_like(ref)

    for g in range(4):
        dq = dot(lt[...], ds[:, g * 256 : (g + 1) * 256], NN).astype(B)
        dqb[2 * g] = dq[:, :PACKET]
        dqb[2 * g + 1] = dq[:, PACKET:]

    def slots(p0, p1):
        return p0 * (1.0 - w0) + p1 * (1.0 - w1), p0 * w0 + p1 * w1

    def arrived(k, p):
        @pl.when(jnp.logical_not(last))
        def _():
            back(k, p).wait_recv()

    @pl.when(jnp.logical_not(first))
    def _():
        for p in parts:
            put(home, (1,), p, middle(1, p))
            back(1, p).start()

    for p in parts:
        arrived(0, p)
        for b, value in enumerate(slots(get(ours, (mm, 1 - hx), p), get(away, (0,), p))):
            put(first_s, (b,), p, value)
            early_send(b, p).start()

    for p in parts:
        mid0 = middle(0, p)
        arrived(1, p)
        for b, value in enumerate(slots(mid0, get(away, (1,), p))):
            put(last_s, (b,), p, value)
            late_send(b, p).start()
    for p in parts:
        for k in range(2):
            early_recv(k, p).wait_recv()
    for p in parts:
        for k in range(2):
            late_recv(k, p).wait_recv()
            value = get(last_r, (k,), p) + get(first_r, (1 - k,), p)
            if p < 2:
                out[k * HALF : (k + 1) * HALF, 256 * p : 256 * p + 256] = value.astype(B)
            else:
                width = KW - LAT
                out[k * HALF : (k + 1) * HALF, LAT:] = jnp.concatenate([value[:, :width], value[:, width:]], axis=0).astype(B)

    @pl.when(jnp.logical_not(last))
    def _():
        for copy in send_lat:
            copy.wait_send()

    @pl.when(jnp.logical_not(first))
    def _():
        for copy in fwd_lat + [pair(2), pair(3)]:
            copy.wait_send()
        for p in parts:
            for k in range(2):
                back(k, p).wait_send()
                owner_send(1, k, p).wait_send()

    for i in range(2):
        pair(i).wait_send()
    for k in range(2):
        for p in parts:
            early_send(k, p).wait_send()
            owner_send(0, k, p).wait_send()
            late_send(k, p).wait_send()


def solution(mesh):
    shards = mesh.shape["seq"]

    def local(queries, out_grad, latents, log_norm, out_delta, plan):
        any_spec = pl.BlockSpec(memory_space=pl.ANY)
        vmem = pl.BlockSpec(memory_space=pltpu.VMEM)
        payloads = []
        for lead, kind in (((4, 2), F), ((2, 2), B), ((2, 2), B)) + (((2,), B),) * 6:
            payloads.append(pltpu.VMEM(lead + (HALF, LAT), kind))
            payloads.append(pltpu.VMEM(lead + (HALF // 2, 128), kind))
        dq, latent_out = pl.pallas_call(
            lambda *refs: kernel(shards, *refs),
            out_shape=(
                pltpu.VMEM((8, KW, PACKET), B),
                pltpu.VMEM((QTR, KW), B),
            ),
            in_specs=[pl.BlockSpec(memory_space=pltpu.SMEM), vmem, vmem, any_spec, any_spec, any_spec],
            out_specs=(vmem, vmem),
            scratch_shapes=[
                pltpu.VMEM((KW, 8 * PACKET), B),
                pltpu.VMEM((PACKET, 8, LAT), B),
                pltpu.VMEM((8 * PACKET, LAT), B),
                pltpu.VMEM((KW, SHARD), B),
                pltpu.VMEM((KW, SHARD), B),
                pltpu.VMEM((SHARD, KW), B),
                pltpu.VMEM((KW // 2, BLOCK), B),
                pltpu.VMEM((SHARD, 8 * PACKET), B),
                pltpu.VMEM((CH, 8 * PACKET), B),
                pltpu.VMEM((CH, KW), F),
                pltpu.VMEM((4, QTR, KW), F),
                pltpu.VMEM((4, QTR, KW), F),
                pltpu.VMEM((4, QTR, KW), F),
                pltpu.SemaphoreType.DMA((10,)),
                pltpu.SemaphoreType.DMA((50,)),
                pltpu.SemaphoreType.DMA((50,)),
            ]
            + payloads,
            compiler_params=pltpu.CompilerParams(
                collective_id=0, has_side_effects=True, vmem_limit_bytes=60 << 20
            ),
            name="mla_bwd",
        )(plan, log_norm.T, out_delta.T, queries.transpose(1, 2, 0), out_grad, latents.T)

        def put(a_ref, b_ref, c_ref, d_ref, sem):
            outs = [pltpu.make_async_copy(a_ref.at[h], c_ref.at[h], sem.at[h]) for h in range(8)]
            outs.append(pltpu.make_async_copy(b_ref, d_ref, sem.at[8]))
            for o in outs:
                o.start()
            for o in outs:
                o.wait()

        dq, latent_out = pl.pallas_call(
            put,
            out_shape=(
                jax.ShapeDtypeStruct((8, KW, PACKET), B),
                jax.ShapeDtypeStruct((QTR, KW), B),
            ),
            in_specs=[vmem, vmem],
            out_specs=(any_spec, any_spec),
            scratch_shapes=[
                pltpu.SemaphoreType.DMA((9,)),
            ],
            compiler_params=pltpu.CompilerParams(vmem_limit_bytes=4 << 20),
            name="mla_put",
        )(dq, latent_out)
        return dq.transpose(2, 0, 1), latent_out

    return jax.shard_map(
        local,
        mesh=mesh,
        in_specs=(
            P("seq", "head", None),
            P("seq", "head", None),
            P("seq", None),
            P("seq", "head"),
            P("seq", "head"),
            P("seq", None),
        ),
        out_specs=(P("seq", "head", None), P(("seq", "head"), None)),
        check_vma=False,
    )
```
